32 devices in a mesh: grp: 4 (over x, core), seq: 8 (over z, y).
Axes of the slice: x: 2, y: 2, z: 4, core: 2. Of those that a mesh axis runs over, the one named last changes fastest.
Arguments:
- spans: bfloat16 [4096, 2048], P(('grp', 'seq')), may hold values from -6 to 6
- span_group: int32 [4096, 1], P(('grp', 'seq')), may hold values from 0 to 3; in each aligned block of 128 rows (0 to 127, 128 to 255, ...) at most 64 rows name the same one
- span_mask: int32 [4096], P(('grp', 'seq')), may hold values 0 or 1
- w_in: bfloat16 [2048, 1024], replicated, may hold values from -0.125 to 0.125
- norm_gain: float32 [2, 1024], replicated, may hold values from 0.25 to 1.75
- w_query: bfloat16 [2, 1024, 1024], replicated, may hold values from -8 to 8
- w_key: bfloat16 [2, 1024, 256], replicated, may hold values from -0.15625 to 0.15625
- w_value: bfloat16 [2, 1024, 256], replicated, may hold values from -0.1875 to 0.1875
- w_out: bfloat16 [2, 1024, 1024], replicated, may hold values from -0.1875 to 0.1875
- final_gain: float32 [1024], replicated, may hold values from 0.25 to 1.75
- w_class: bfloat16 [1024, 256], replicated, may hold values from -0.1875 to 0.1875
Outputs:
- hidden: bfloat16 [8192, 1024], P(('grp', 'seq'))
- logits: float32 [4, 256], P('grp')
The draws below stay inside these ranges and needn't reach their ends.
Inputs may be any that keep to these rules, and one draw needn't show every extreme that they name: `span_group`: among the 128 spans of one device, at most 64 belong to one document; some device has exactly 64 for some document.
All inputs are finite; a program needn't handle non-finite values. No bound on the sum of `span_mask` on one device may be relied on, other than what follows from the above.
Results may differ from the reference program's by a relative error of at most 0.009.
Values may be sent and summed in bfloat16 or wider, within the bound.
No kernel may reach another device: no remote copies, remote signals or barrier semaphores. Data moves between devices by JAX's collectives and lax.ppermute only.
A program may use at most 192 MiB of HBM per device.

```python
import math
import jax
import jax.numpy as jnp
import numpy as np
from jax import lax

EMB = 2048
D = 1024
HEADS = 16
HDIM = 64
KV_HEADS = 4
CLASSES = 256
LAYERS = 2
ROW_DEV = 128
CAP = 64
SLOTS = 256
GROUP_ROWS = 2048
SPANS = 4096
N_GRP = 4
N_SEQ = 8


def drawn_heads(key):
    return jax.random.randint(jax.random.fold_in(key, 13), (LAYERS,), 0, KV_HEADS)


def base_entries(key, shape):
    drawn = jnp.clip(jax.random.normal(key, shape, jnp.float32), -4.0, 4.0)
    return drawn * D ** (-0.5)


def query_base(key):
    return base_entries(jax.random.fold_in(key, 11), (LAYERS, D, HEADS * HDIM))


def draw_w_query(key, part):
    base = query_base(key)
    chosen = drawn_heads(key)
    group = HEADS // KV_HEADS
    column = jnp.arange(HEADS * HDIM, dtype=jnp.int32)
    strength = 256.0 * (1.0 + jnp.arange(LAYERS, dtype=jnp.float32)) * HDIM ** (-0.5)
    hit = column[None, :] // HDIM == chosen[:, None] * group
    factor = jnp.where(hit, strength[:, None], 1.0)
    return (base * factor[:, None, :]).astype(jnp.bfloat16)


def draw_w_key(key, part):
    base = query_base(key)
    chosen = drawn_heads(key)
    group = HEADS // KV_HEADS
    shape = (LAYERS, D, KV_HEADS * HDIM)
    noise = base_entries(jax.random.fold_in(key, 12), shape)
    column = jnp.arange(KV_HEADS * HDIM, dtype=jnp.int32)
    source = chosen[:, None] * group * HDIM + column[None, :] % HDIM
    picked = jnp.take_along_axis(base, jnp.broadcast_to(source[:, None, :], shape), axis=2)
    hit = column[None, :] // HDIM == chosen[:, None]
    mixed = jnp.where(hit[:, None, :], 0.9 * picked + 0.3 * noise, noise)
    return mixed.astype(jnp.bfloat16)


def draw_spans(key, part):
    shape = (SPANS, EMB)
    drawn = jnp.clip(jax.random.normal(jax.random.fold_in(key, 21), shape, jnp.float32), -6.0, 6.0)
    return drawn.astype(jnp.bfloat16)


def plant(result, stream_key, low, top_value):
    longest = result.shape.index(max(result.shape))
    spots = []
    for shift in (0, 1):
        where = [jax.random.randint(jax.random.fold_in(stream_key, axis), (), 0, length) for axis, length in enumerate(result.shape)]
        where[longest] = (where[longest] + shift) % result.shape[longest]
        spots.append(tuple(where))
    return result.at[spots[0]].set(low).at[spots[1]].set(top_value)


def routed_block(own_key, own, number, rows, amount, top, reach, slope):
    ranking = jax.random.permutation(own_key, amount)
    heavy_load, ordinary = shares(amount, rows * top, reach, slope, True), shares(amount, rows * top, reach, slope, False)
    places = jnp.arange(amount)

    def named(sizes, turn):
        used = int((sizes > 0).sum())
        fixed = max(1, used // 4)
        moved = fixed + (places - fixed + turn * (used - fixed)) % max(1, amount - fixed)
        return jnp.zeros((amount,), jnp.int32).at[ranking[jnp.where(places < fixed, places, moved)]].set(jnp.asarray(sizes, jnp.int32))

    sizes = jnp.where(number % 4 == 0, named(heavy_load, number // 4), named(ordinary, number - number // 4 - 1))
    mixed = jax.random.permutation(jax.random.fold_in(own, 3), amount)
    donor, receiver = mixed[0:amount // 2 * 2:2], mixed[1:amount // 2 * 2:2]
    margin = jnp.minimum(sizes[donor] - 1, reach - sizes[receiver]) // 2
    margin = jnp.where((donor == ranking[0]) | (receiver == ranking[0]) | (sizes[receiver] == 0), 0, jnp.maximum(margin, 0))
    moved = jax.random.randint(jax.random.fold_in(own, 4), (amount // 2,), 0, 1 << 20) % (margin + 1)
    sizes = sizes.at[donor].add(-moved).at[receiver].add(moved)
    labels = jnp.searchsorted(jnp.cumsum(sizes), jnp.arange(rows * top), side="right").astype(jnp.int32)
    grid = labels.reshape(top, rows).T
    grid = grid[jax.random.permutation(jax.random.fold_in(own, 1), rows)]
    turn = jax.random.randint(jax.random.fold_in(own, 2), (rows, 1), 0, top)
    return jnp.take_along_axis(grid, (jnp.arange(top)[None, :] + turn) % top, axis=1)


def shares(amount, total, most, slope, full):
    portions = [(1 << 20) // math.isqrt(rank ** slope) + 1 for rank in range(1, amount + 1)]
    largest = most if full else min(most, max(-(-total // amount), total * portions[0] // sum(portions)))
    least = 1 if total - largest >= amount - 1 else 0
    given, spare = [largest] + [least] * (amount - 1), total - largest - least * (amount - 1)
    while spare > 0:
        free = [i for i in range(1, amount) if given[i] < largest] or [i for i in range(1, amount) if given[i] < most]
        pool, remaining = sum([portions[i] for i in free]), spare
        for i in free:
            addition = min(most - given[i], max(1, remaining * portions[i] // pool), spare)
            given[i] = given[i] + addition
            spare = spare - addition
    return np.array(given)


def centred(rng, extent, spread, bound, kind=jnp.bfloat16):
    entries = jax.random.normal(rng, extent, jnp.float32) * spread
    return jnp.minimum(jnp.maximum(entries, -bound), bound).astype(kind)


def setup_inputs(seed: int = 0) -> dict:
    seeds = jax.random.split(jax.random.key(seed), 12)
    spans = draw_spans(jax.random.fold_in(seeds[11], 71), 0)
    span_group_keys = jax.random.split(jax.random.fold_in(seeds[1], 1), SPANS // ROW_DEV)
    span_group_turns = jax.random.permutation(jax.random.fold_in(seeds[1], 3), SPANS // ROW_DEV)
    span_group = jax.vmap(lambda own, number: routed_block(jax.random.fold_in(seeds[1], 2), own, number, ROW_DEV, N_GRP, 1, CAP, 2))(span_group_keys, span_group_turns).reshape((SPANS, 1))
    span_mask = plant((jax.random.randint(seeds[2], (SPANS,), 0, 8) < 7).astype(jnp.int32), jax.random.fold_in(seeds[2], 1), 0, 1)
    w_in = centred(seeds[3], (EMB, D), EMB ** -0.5, 0.125)
    norm_gain = jnp.clip(1.0 + 0.15 * jax.random.normal(seeds[4], (LAYERS, D), jnp.float32), 0.25, 1.75)
    w_query = draw_w_query(jax.random.fold_in(seeds[11], 71), 0)
    w_key = draw_w_key(jax.random.fold_in(seeds[11], 71), 0)
    w_value = centred(seeds[7], (LAYERS, D, KV_HEADS * HDIM), D ** -0.5, 0.1875)
    w_out = centred(seeds[8], (LAYERS, HEADS * HDIM, D), (HEADS * HDIM) ** -0.5, 0.1875)
    final_gain = jnp.clip(1.0 + 0.15 * jax.random.normal(seeds[9], (D,), jnp.float32), 0.25, 1.75)
    w_class = centred(seeds[10], (D, CLASSES), D ** -0.5, 0.1875)
    return {"spans": spans, "span_group": span_group, "span_mask": span_mask, "w_in": w_in, "norm_gain": norm_gain, "w_query": w_query, "w_key": w_key, "w_value": w_value, "w_out": w_out, "final_gain": final_gain, "w_class": w_class}


def attend(query, keys, values, valid):
    group = HEADS // KV_HEADS
    rows = query.shape[0]
    scale = HDIM ** (-0.5)
    pieces = []
    for head in range(KV_HEADS):
        q_block = query[:, head * group * HDIM:(head + 1) * group * HDIM].reshape(rows, group, HDIM).astype(jnp.float32)
        k_block = keys[:, head * HDIM:(head + 1) * HDIM].astype(jnp.float32)
        v_block = values[:, head * HDIM:(head + 1) * HDIM].astype(jnp.float32)
        scores = jnp.einsum('rgd,kd->rgk', q_block, k_block) * scale
        scores = jnp.where(valid[None, None, :] > 0, scores, -1e+30)
        top = lax.optimization_barrier(jnp.max(scores, axis=-1, keepdims=True))
        weight = jnp.exp(scores - top)
        total = lax.optimization_barrier(jnp.sum(weight, axis=-1, keepdims=True))
        rounded = weight.astype(jnp.bfloat16).astype(jnp.float32)
        out = jnp.einsum('rgk,kd->rgd', rounded, v_block) / total
        pieces.append(out.reshape(rows, group * HDIM))
    return jnp.concatenate(pieces, axis=1).astype(jnp.bfloat16)

def reference(spans, span_group, span_mask, w_in, norm_gain, w_query, w_key, w_value, w_out, final_gain, w_class):
    blocks = N_GRP * N_SEQ
    target = span_group[:, 0].reshape(blocks, ROW_DEV)
    member = (target[:, :, None] == jnp.arange(N_GRP, dtype=jnp.int32)[None, None, :]).astype(jnp.int32)
    rank = lax.optimization_barrier(jnp.sum(jnp.cumsum(member, axis=1) * member, axis=2)) - 1
    source = jnp.arange(blocks, dtype=jnp.int32)[:, None]
    place = source % N_SEQ * SLOTS + source // N_SEQ * CAP + rank
    flat = (target * GROUP_ROWS + place).reshape(-1).astype(jnp.int32)
    projected = jnp.dot(spans, w_in, preferred_element_type=jnp.float32).astype(jnp.bfloat16)
    states = jnp.zeros((N_GRP * GROUP_ROWS, D), jnp.bfloat16).at[flat].set(projected)
    valid = jnp.zeros((N_GRP * GROUP_ROWS,), jnp.float32).at[flat].set(span_mask.astype(jnp.float32))
    states = states.reshape(N_GRP, GROUP_ROWS, D)
    valid = valid.reshape(N_GRP, GROUP_ROWS)

    def one_document(pair):
        current, mask = pair
        for layer in range(LAYERS):
            xf = current.astype(jnp.float32)
            normed = (xf * lax.rsqrt(lax.optimization_barrier(jnp.mean(xf * xf, axis=-1, keepdims=True)) + 1e-05) * norm_gain[layer]).astype(jnp.bfloat16)
            query = jnp.dot(normed, w_query[layer], preferred_element_type=jnp.float32).astype(jnp.bfloat16)
            keys = jnp.dot(normed, w_key[layer], preferred_element_type=jnp.float32).astype(jnp.bfloat16)
            values = jnp.dot(normed, w_value[layer], preferred_element_type=jnp.float32).astype(jnp.bfloat16)
            attended = attend(query, keys, values, mask)
            current = (xf + jnp.dot(attended, w_out[layer], preferred_element_type=jnp.float32)).astype(jnp.bfloat16)
        final = current.astype(jnp.float32)
        hidden_doc = jnp.where(mask[:, None] > 0, current, jnp.zeros_like(current))
        pooled = lax.optimization_barrier(jnp.sum(mask[:, None] * final, axis=0))
        summary = (pooled * lax.rsqrt(jnp.mean(pooled * pooled) + 1e-05) * final_gain).astype(jnp.bfloat16)
        scores = jnp.dot(summary[None, :], w_class, preferred_element_type=jnp.float32)[0]
        return (hidden_doc, scores)
    hidden, logits = lax.map(one_document, (states, valid))
    return (hidden.reshape(N_GRP * GROUP_ROWS, D), logits)
```

```python
import functools

import jax
import jax.numpy as jnp
from jax import lax
from jax.experimental import pallas as pl
from jax.experimental.pallas import tpu as pltpu
from jax.sharding import PartitionSpec as P

HEADS = 16
HDIM = 64
KV_HEADS = 4
KV = KV_HEADS * HDIM
LANES = 128
EXTRA = 8
FAR = -1e30


def attend_kernel(stacked, carried, last, *refs):
    count = len(stacked)
    q_ref, doc_ref, far_ref = refs[:3]
    blocks = refs[3 : 3 + count]
    refs = refs[3 + count :]
    if carried:
        acc_in, stat_in = refs[:2]
        refs = refs[2:]
    if last:
        out_ref, ka, va = refs
    else:
        acc_out, stat_out, ka, va = refs
    rows = q_ref.shape[0]
    lane = lax.broadcasted_iota(jnp.int32, (rows, LANES), 1)
    low = lane < HDIM
    ka[:, LANES:] = far_ref[...]
    va[:, LANES:] = jnp.ones((va.shape[0], LANES), jnp.bfloat16)
    stats = jnp.zeros((rows, LANES), jnp.float32)
    doc = doc_ref[...]
    for pair in range(KV_HEADS // 2):
        at = 0
        for block, number in zip(blocks, stacked):
            for i in range(max(number, 1)):
                view = block.at[i] if number else block
                ka[at : at + rows, :LANES] = view[:rows, pair * LANES : (pair + 1) * LANES]
                va[at : at + rows, :LANES] = view[
                    :rows, KV + pair * LANES : KV + (pair + 1) * LANES
                ]
                at += rows
        for step in range(HEADS // 4):
            head = pair * (HEADS // 2) + 2 * step
            upper = head // (HEADS // KV_HEADS) % 2
            columns = slice(head * HDIM, head * HDIM + LANES)
            both = q_ref[:, columns].astype(jnp.float32)
            turned = pltpu.roll(both, HDIM, 1)
            first, second = (turned, both) if upper else (both, turned)
            keep = ~low if upper else low
            first = jnp.where(keep, first, 0.0).astype(jnp.bfloat16)
            second = jnp.where(keep, second, 0.0).astype(jnp.bfloat16)
            queries = jnp.concatenate(
                [jnp.concatenate([first, doc], 1), jnp.concatenate([second, doc], 1)], 0
            )
            scores = lax.dot_general(
                queries, ka[...], (((1,), (1,)), ((), ())), preferred_element_type=jnp.float32
            )
            top = jnp.max(scores, axis=1, keepdims=True)
            if carried:
                before = jnp.concatenate(
                    [stat_in[:, head : head + 1], stat_in[:, head + 1 : head + 2]], 0
                )
                top = jnp.maximum(top, before)
                shrink = jnp.exp(before - top)
            weight = jnp.exp(scores - top).astype(jnp.bfloat16)
            product = jnp.dot(weight, va[...], preferred_element_type=jnp.float32)
            total = product[:, LANES:]
            if upper:
                block = jnp.where(low, pltpu.roll(product[:rows, :LANES], HDIM, 1), product[rows:, :LANES])
            else:
                block = jnp.where(low, product[:rows, :LANES], pltpu.roll(product[rows:, :LANES], HDIM, 1))
            total = jnp.where(low, total[:rows], total[rows:])
            if carried:
                factor = jnp.where(low, shrink[:rows], shrink[rows:])
                block = block + factor * acc_in[:, columns]
                old = jnp.where(
                    low,
                    stat_in[:, HDIM + head : HDIM + head + 1],
                    stat_in[:, HDIM + head + 1 : HDIM + head + 2],
                )
                total = total + factor * old
            if last:
                out_ref[:, columns] = (block / total).astype(jnp.bfloat16)
            else:
                acc_out[:, columns] = block
                stats = jnp.where(lane == head, top[:rows], stats)
                stats = jnp.where(lane == head + 1, top[rows:], stats)
                stats = jnp.where(lane == HDIM + head, total[:, :1], stats)
                stats = jnp.where(lane == HDIM + head + 1, total[:, HDIM : HDIM + 1], stats)
    if not last:
        stat_out[...] = stats


def attend(query, doc, far, blocks, carry, last):
    rows, width = query.shape
    stacked = tuple(b.shape[0] if b.ndim == 3 else 0 for b in blocks)
    keys = rows * sum(max(n, 1) for n in stacked)
    if last:
        out = jax.ShapeDtypeStruct((rows, width), jnp.bfloat16)
    else:
        out = (
            jax.ShapeDtypeStruct((rows, width), jnp.float32),
            jax.ShapeDtypeStruct((rows, LANES), jnp.float32),
        )
    carried = () if carry is None else carry
    return pl.pallas_call(
        functools.partial(attend_kernel, stacked, carry is not None, last),
        out_shape=out,
        scratch_shapes=[
            pltpu.VMEM((keys, 2 * LANES), jnp.bfloat16),
            pltpu.VMEM((keys, 2 * LANES), jnp.bfloat16),
        ],
        compiler_params=pltpu.CompilerParams(vmem_limit_bytes=56 * 1024 * 1024),
        cost_estimate=pl.CostEstimate(
            flops=4 * rows * keys * width,
            bytes_accessed=keys * 4 * KV,
            transcendentals=rows * keys * HEADS,
        ),
        name="attend",
    )(query, doc, far, *blocks, *carried)


def across(array, axis, bit):
    size = lax.axis_size(axis)
    return lax.ppermute(array, axis, [(i, i ^ bit) for i in range(size)])


def gather_blocks(block):
    grp, seq = lax.axis_size("grp"), lax.axis_size("seq")
    if (grp, seq) != (4, 8):
        whole = lax.all_gather(block, ("grp", "seq"), axis=0, tiled=False)
        part = 32 if whole.shape[0] % 32 == 0 else whole.shape[0]
        return [[whole[i : i + part]] for i in range(0, whole.shape[0], part)]
    line = [block] + [across(block, "seq", bit) for bit in (2, 4, 6)]
    side = [across(b, "grp", 2) for b in line]
    flat = [across(b, "seq", 1) for b in line]
    corner = [across(b, "grp", 2) for b in flat[:2]] + [across(b, "seq", 1) for b in side[2:]]
    groups = (line, side, flat, corner)
    other = [across(jnp.stack(g), "grp", 1) for g in groups]
    return [[b for g in groups for b in g] + other]


def placement(code, lanes):
    return jnp.where(code[:, None] == lanes[None, :], 0.0, FAR).astype(jnp.bfloat16)


def per_device(
    spans,
    span_group,
    span_mask,
    w_in,
    norm_gain,
    w_query,
    w_key,
    w_value,
    w_out,
    final_gain,
    w_class,
):
    rows = spans.shape[0]
    groups = lax.axis_size("grp")
    capacity = 2 * rows // groups
    slots = groups * capacity
    target = span_group[:, 0]
    number = jnp.arange(rows, dtype=jnp.int32)
    earlier = (number[None, :] < number[:, None]) & (target[None, :] == target[:, None])
    rank = jnp.sum(earlier.astype(jnp.int32), axis=1)
    slot_of = target * capacity + rank
    placing = (jnp.arange(slots, dtype=jnp.int32)[:, None] == slot_of[None, :]) & (
        span_mask[None, :] > 0
    )
    placing = placing.astype(jnp.bfloat16)
    lanes = jnp.arange(LANES, dtype=jnp.int32)
    doc = (target[:, None] == lanes[None, :]).astype(jnp.bfloat16)
    code = jnp.where(span_mask > 0, target, LANES).astype(jnp.bfloat16)
    states = jnp.dot(spans, w_in, preferred_element_type=jnp.float32).astype(jnp.bfloat16)
    far = None
    for layer in range(w_query.shape[0]):
        xf = states.astype(jnp.float32)
        normed = (
            xf * lax.rsqrt(jnp.mean(xf * xf, axis=-1, keepdims=True) + 1e-05) * norm_gain[layer]
        ).astype(jnp.bfloat16)
        keys = jnp.dot(normed, w_key[layer], preferred_element_type=jnp.float32)
        values = jnp.dot(normed, w_value[layer], preferred_element_type=jnp.float32)
        block = jnp.concatenate([keys, values], axis=1).astype(jnp.bfloat16)
        if layer == 0:
            tail = jnp.broadcast_to(jnp.pad(code, (0, 2 * KV - rows))[None, :], (EXTRA, 2 * KV))
            block = jnp.concatenate([block, tail], axis=0)
        query = jnp.dot(normed, w_query[layer], preferred_element_type=jnp.float32).astype(
            jnp.bfloat16
        )
        query = query * jnp.bfloat16(HDIM**-0.5)
        stages = gather_blocks(block)
        if far is None:
            far = []
            for stage in stages:
                codes = [
                    b[..., rows, :rows].reshape(-1) for b in stage
                ]
                far.append(placement(jnp.concatenate(codes).astype(jnp.int32), lanes))
        carry = None
        for i, stage in enumerate(stages):
            carry = attend(query, doc, far[i], stage, carry, i == len(stages) - 1)
        states = (xf + jnp.dot(carry, w_out[layer], preferred_element_type=jnp.float32)).astype(
            jnp.bfloat16
        )
    packed = jnp.dot(placing, states, preferred_element_type=jnp.float32).astype(jnp.bfloat16)
    packed = packed.reshape(groups, capacity, states.shape[1])
    hidden = lax.all_to_all(packed, "grp", split_axis=0, concat_axis=0, tiled=True)
    hidden = hidden.reshape(slots, states.shape[1])
    local_sum = jnp.sum(hidden.astype(jnp.float32), axis=0)
    size = lax.axis_size("seq")
    sums = lax.all_to_all(
        jnp.broadcast_to(local_sum[None, :], (size, local_sum.shape[0])),
        "seq",
        split_axis=0,
        concat_axis=0,
        tiled=True,
    )
    pooled = jnp.sum(sums, axis=0)
    summary = (pooled * lax.rsqrt(jnp.mean(pooled * pooled) + 1e-05) * final_gain).astype(
        jnp.bfloat16
    )
    logits = jnp.dot(summary[None, :], w_class, preferred_element_type=jnp.float32)
    return (hidden, logits)


def solution(mesh):
    return jax.shard_map(
        per_device,
        mesh=mesh,
        in_specs=(
            P(("grp", "seq"), None),
            P(("grp", "seq"), None),
            P(("grp", "seq")),
            P(),
            P(),
            P(),
            P(),
            P(),
            P(),
            P(),
            P(),
        ),
        out_specs=(P(("grp", "seq"), None), P("grp", None)),
        check_vma=False,
    )
```

```python
import functools

import jax
import jax.numpy as jnp
from jax import lax
from jax.experimental import pallas as pl
from jax.experimental.pallas import tpu as pltpu
from jax.sharding import PartitionSpec as P

HEADS = 16
HDIM = 64
KV_HEADS = 4
KV = KV_HEADS * HDIM
LANES = 128
EXTRA = 8
FAR = -1e30


def attend_kernel(stacked, coded, carried, last, *refs):
    count = len(stacked)
    q_ref, doc_ref = refs[:2]
    blocks = refs[2 : 2 + count]
    refs = refs[2 + count :]
    if not coded:
        far_ref, refs = refs[0], refs[1:]
    if carried:
        acc_in, stat_in = refs[:2]
        refs = refs[2:]
    if coded:
        far_ref, refs = refs[0], refs[1:]
    if last:
        out_ref, ka, va = refs
    else:
        acc_out, stat_out, ka, va = refs
    rows = q_ref.shape[0]
    lane = lax.broadcasted_iota(jnp.int32, (rows, LANES), 1)
    low = lane < HDIM
    if coded:
        at = 0
        line = lax.broadcasted_iota(jnp.int32, (LANES, rows), 0).astype(jnp.float32)
        same = (lax.broadcasted_iota(jnp.int32, (rows, rows), 0) == lax.broadcasted_iota(jnp.int32, (rows, rows), 1))
        same = jnp.where(same, 1.0, 0.0).astype(jnp.bfloat16)
        for block, number in zip(blocks, stacked):
            for i in range(max(number, 1)):
                view = block.at[i] if number else block
                code = view[rows : rows + EXTRA, :rows].astype(jnp.float32)[:1]
                across_keys = jnp.where(line == code, 0.0, FAR).astype(jnp.bfloat16)
                far_ref[at : at + rows, :] = lax.dot_general(
                    same, across_keys, (((1,), (1,)), ((), ())), preferred_element_type=jnp.float32
                ).astype(jnp.bfloat16)
                at += rows
    ka[:, LANES:] = far_ref[...]
    va[:, LANES:] = jnp.ones((va.shape[0], LANES), jnp.bfloat16)
    stats = jnp.zeros((rows, LANES), jnp.float32)
    doc = doc_ref[...]
    for pair in range(KV_HEADS // 2):
        at = 0
        for block, number in zip(blocks, stacked):
            for i in range(max(number, 1)):
                view = block.at[i] if number else block
                ka[at : at + rows, :LANES] = view[:rows, pair * LANES : (pair + 1) * LANES]
                va[at : at + rows, :LANES] = view[
                    :rows, KV + pair * LANES : KV + (pair + 1) * LANES
                ]
                at += rows
        for step in range(HEADS // 4):
            head = pair * (HEADS // 2) + 2 * step
            upper = head // (HEADS // KV_HEADS) % 2
            columns = slice(head * HDIM, head * HDIM + LANES)
            both = q_ref[:, columns].astype(jnp.float32)
            turned = pltpu.roll(both, HDIM, 1)
            first, second = (turned, both) if upper else (both, turned)
            keep = ~low if upper else low
            first = jnp.where(keep, first, 0.0).astype(jnp.bfloat16)
            second = jnp.where(keep, second, 0.0).astype(jnp.bfloat16)
            queries = jnp.concatenate(
                [jnp.concatenate([first, doc], 1), jnp.concatenate([second, doc], 1)], 0
            )
            scores = lax.dot_general(
                queries, ka[...], (((1,), (1,)), ((), ())), preferred_element_type=jnp.float32
            )
            top = jnp.max(scores, axis=1, keepdims=True)
            if carried:
                before = jnp.concatenate(
                    [stat_in[:, head : head + 1], stat_in[:, head + 1 : head + 2]], 0
                )
                top = jnp.maximum(top, before)
                shrink = jnp.exp(before - top)
            weight = jnp.exp(scores - top).astype(jnp.bfloat16)
            product = jnp.dot(weight, va[...], preferred_element_type=jnp.float32)
            total = product[:, LANES:]
            if upper:
                block = jnp.where(low, pltpu.roll(product[:rows, :LANES], HDIM, 1), product[rows:, :LANES])
            else:
                block = jnp.where(low, product[:rows, :LANES], pltpu.roll(product[rows:, :LANES], HDIM, 1))
            total = jnp.where(low, total[:rows], total[rows:])
            if carried:
                factor = jnp.where(low, shrink[:rows], shrink[rows:])
                block = block + factor * acc_in[:, columns]
                old = jnp.where(
                    low,
                    stat_in[:, HDIM + head : HDIM + head + 1],
                    stat_in[:, HDIM + head + 1 : HDIM + head + 2],
                )
                total = total + factor * old
            if last:
                out_ref[:, columns] = (block / total).astype(jnp.bfloat16)
            else:
                acc_out[:, columns] = block
                stats = jnp.where(lane == head, top[:rows], stats)
                stats = jnp.where(lane == head + 1, top[rows:], stats)
                stats = jnp.where(lane == HDIM + head, total[:, :1], stats)
                stats = jnp.where(lane == HDIM + head + 1, total[:, HDIM : HDIM + 1], stats)
    if not last:
        stat_out[...] = stats


def attend(query, doc, far, blocks, carry, last):
    rows, width = query.shape
    stacked = tuple(b.shape[0] if b.ndim == 3 else 0 for b in blocks)
    keys = rows * sum(max(n, 1) for n in stacked)
    out = () if far is not None else (jax.ShapeDtypeStruct((keys, LANES), jnp.bfloat16),)
    if last:
        out = out + (jax.ShapeDtypeStruct((rows, width), jnp.bfloat16),)
    else:
        out = out + (
            jax.ShapeDtypeStruct((rows, width), jnp.float32),
            jax.ShapeDtypeStruct((rows, LANES), jnp.float32),
        )
    carried = () if carry is None else carry
    given = () if far is None else (far,)
    out = pl.pallas_call(
        functools.partial(attend_kernel, stacked, far is None, carry is not None, last),
        out_shape=out,
        scratch_shapes=[
            pltpu.VMEM((keys, 2 * LANES), jnp.bfloat16),
            pltpu.VMEM((keys, 2 * LANES), jnp.bfloat16),
        ],
        compiler_params=pltpu.CompilerParams(vmem_limit_bytes=56 * 1024 * 1024),
        cost_estimate=pl.CostEstimate(
            flops=4 * rows * keys * width,
            bytes_accessed=keys * 4 * KV,
            transcendentals=rows * keys * HEADS,
        ),
        name="attend",
    )(query, doc, *blocks, *given, *carried)
    if far is None:
        far, out = out[0], out[1:]
    return far, out[0] if last else out


def across(array, axis, bit):
    size = lax.axis_size(axis)
    return lax.ppermute(array, axis, [(i, i ^ bit) for i in range(size)])


def gather_blocks(block):
    grp, seq = lax.axis_size("grp"), lax.axis_size("seq")
    if (grp, seq) != (4, 8):
        whole = lax.all_gather(block, ("grp", "seq"), axis=0, tiled=False)
        part = 32 if whole.shape[0] % 32 == 0 else whole.shape[0]
        return [[whole[i : i + part]] for i in range(0, whole.shape[0], part)]
    line = [block] + [across(block, "seq", bit) for bit in (2, 4, 6)]
    side = [across(b, "grp", 2) for b in line]
    flat = [across(b, "seq", 1) for b in line]
    corner = [across(b, "grp", 2) for b in flat[:2]] + [across(b, "seq", 1) for b in side[2:]]
    groups = (line, side, flat, corner)
    other = [across(jnp.stack(g), "grp", 1) for g in groups]
    return [[b for g in groups for b in g] + other]


def route(packed, near):
    groups = packed.shape[0]
    if groups != 4:
        return lax.all_to_all(packed, "grp", split_axis=0, concat_axis=0, tiled=True)
    came = [packed[0]] + [across(packed[bit], "grp", bit) for bit in range(1, groups)]
    flip = (near & 1) > 0
    came = [jnp.where(flip, came[i ^ 1], came[i]) for i in range(groups)]
    flip = (near & 2) > 0
    return jnp.stack([jnp.where(flip, came[i ^ 2], came[i]) for i in range(groups)])


def per_device(
    spans,
    span_group,
    span_mask,
    w_in,
    norm_gain,
    w_query,
    w_key,
    w_value,
    w_out,
    final_gain,
    w_class,
):
    rows = spans.shape[0]
    groups = lax.axis_size("grp")
    capacity = 2 * rows // groups
    slots = groups * capacity
    target = span_group[:, 0]
    number = jnp.arange(rows, dtype=jnp.int32)
    earlier = (number[None, :] < number[:, None]) & (target[None, :] == target[:, None])
    rank = jnp.sum(earlier.astype(jnp.int32), axis=1)
    near = lax.axis_index("grp") if groups == 4 else 0
    slot_of = (target ^ near) * capacity + rank
    placing = (jnp.arange(slots, dtype=jnp.int32)[:, None] == slot_of[None, :]) & (
        span_mask[None, :] > 0
    )
    placing = placing.astype(jnp.bfloat16)
    counted = (jnp.arange(groups, dtype=jnp.int32)[:, None] == target[None, :]) & (
        span_mask[None, :] > 0
    )
    counted = counted.astype(jnp.bfloat16)
    lanes = jnp.arange(LANES, dtype=jnp.int32)
    doc = (target[:, None] == lanes[None, :]).astype(jnp.bfloat16)
    code = jnp.where(span_mask > 0, target, LANES).astype(jnp.bfloat16)
    states = jnp.dot(spans, w_in, preferred_element_type=jnp.float32).astype(jnp.bfloat16)
    far = []
    for layer in range(w_query.shape[0]):
        xf = states.astype(jnp.float32)
        normed = (
            xf * lax.rsqrt(jnp.mean(xf * xf, axis=-1, keepdims=True) + 1e-05) * norm_gain[layer]
        ).astype(jnp.bfloat16)
        keys = jnp.dot(normed, w_key[layer], preferred_element_type=jnp.float32)
        values = jnp.dot(normed, w_value[layer], preferred_element_type=jnp.float32)
        block = jnp.concatenate([keys, values], axis=1).astype(jnp.bfloat16)
        if layer == 0:
            tail = jnp.broadcast_to(jnp.pad(code, (0, 2 * KV - rows))[None, :], (EXTRA, 2 * KV))
            block = jnp.concatenate([block, tail], axis=0)
        query = jnp.dot(normed, w_query[layer], preferred_element_type=jnp.float32).astype(
            jnp.bfloat16
        )
        query = query * jnp.bfloat16(HDIM**-0.5)
        stages = gather_blocks(block)
        carry = None
        for i, stage in enumerate(stages):
            given = far[i] if layer else None
            kept, carry = attend(query, doc, given, stage, carry, i == len(stages) - 1)
            if not layer:
                far.append(kept)
        states = (xf + jnp.dot(carry, w_out[layer], preferred_element_type=jnp.float32)).astype(
            jnp.bfloat16
        )
    packed = jnp.dot(placing, states, preferred_element_type=jnp.float32).astype(jnp.bfloat16)
    packed = packed.reshape(groups, capacity, states.shape[1])
    parts = jnp.dot(counted, states, preferred_element_type=jnp.float32)
    hidden = route(packed, near)
    hidden = hidden.reshape(slots, states.shape[1])
    size = lax.axis_size("seq")
    sums = lax.all_to_all(
        jnp.broadcast_to(parts[:, None, :], (groups, size, parts.shape[1])).reshape(
            groups * size, parts.shape[1]
        ),
        ("grp", "seq"),
        split_axis=0,
        concat_axis=0,
        tiled=True,
    )
    pooled = jnp.sum(sums, axis=0)
    summary = (pooled * lax.rsqrt(jnp.mean(pooled * pooled) + 1e-05) * final_gain).astype(
        jnp.bfloat16
    )
    logits = jnp.dot(summary[None, :], w_class, preferred_element_type=jnp.float32)
    return (hidden, logits)


def solution(mesh):
    return jax.shard_map(
        per_device,
        mesh=mesh,
        in_specs=(
            P(("grp", "seq"), None),
            P(("grp", "seq"), None),
            P(("grp", "seq")),
            P(),
            P(),
            P(),
            P(),
            P(),
            P(),
            P(),
            P(),
        ),
        out_specs=(P(("grp", "seq"), None), P("grp", None)),
        check_vma=False,
    )
```
